256 devices in a mesh: region: 4 (over y), shard: 64 (over x, z, core).
Axes of the slice: x: 4, y: 4, z: 8, core: 2. Of those that a mesh axis runs over, the one named last changes fastest.
Arguments:
- features: bfloat16 [65536, 1024], P(('region', 'shard')), may hold values from -6 to 6
- proj_weight: bfloat16 [1024, 1024], replicated, may hold values from -0.1875 to 0.1875
- proj_bias: float32 [1024], replicated, may hold values from -3 to 3
- self_weight: bfloat16 [1024, 1024], replicated, may hold values from -0.1875 to 0.1875
- nbr_weight: bfloat16 [1024, 1024], replicated, may hold values from -0.1875 to 0.1875
- out_bias: float32 [1024], replicated, may hold values from -3 to 3
- nbr_ids: int32 [65536, 8], P(('region', 'shard')), may hold values from 0 to 16383, as said below
- nbr_counts: int32 [65536, 8], P(('region', 'shard')), may hold values from 1 to 32
- live_slots: int32 [512], P(('region', 'shard')), may hold values from 1 to 8
- query_ids: int32 [16384], P(('region', 'shard')), may hold values from 0 to 255
- positive_ids: int32 [16384], P(('region', 'shard')), may hold values from 0 to 255
- neg_blocks: int32 [256, 4], P(('region', 'shard')), may hold values from 0 to 7, as said below
Outputs:
- embedding: bfloat16 [65536, 1024], P(('region', 'shard'))
- hinge_terms: float32 [16384, 4], P(('region', 'shard'))
The draws below stay inside these ranges and needn't reach their ends.
Inputs may be any that keep to these rules, and one draw needn't show every extreme that they name: `nbr_ids`: entries index items of the item's own region. Of the 2048 neighbour slots of one device, at most 64 name items held by any one device, and exactly 64 name the items of one device. `neg_blocks`: entry g names block g % 2 of the device at the same shard index in region g // 2; never a block of the device's own region.
All inputs are finite; a program needn't handle non-finite values.
Results may differ from the reference program's by a relative error of at most 0.0036.
Values may be sent and summed in bfloat16 or wider, within the bound.
A program may use at most 128 MiB of HBM per device.

```python
import jax
import jax.numpy as jnp
from jax import lax

D = 1024
H = 1024
BLOCK = 128
K = 8
NB = 4
ITEM_DEV = 256
QD = 64
BLK_DEV = 2
ITEMS = 65536
QUERIES = 16384
CAP = 64
N_REGION = 4
N_SHARD = 64


def draw_nbr_ids(key, part):
    device_count = N_REGION * N_SHARD
    slots = ITEM_DEV * K

    def single_device(device_key):
        hot_key, perm_key, row_key = jax.random.split(device_key, 3)
        hottest = jax.random.randint(hot_key, (), 0, N_SHARD)
        position = jnp.arange(slots, dtype=jnp.int32)
        others = (hottest + 1 + (position - CAP) % (N_SHARD - 1)) % N_SHARD
        owners = jnp.where(position < CAP, hottest, others)
        owners = owners[jax.random.permutation(perm_key, slots)]
        item_rows = jax.random.randint(row_key, (slots,), 0, ITEM_DEV)
        return (owners * ITEM_DEV + item_rows).reshape(ITEM_DEV, K)
    keys = jax.random.split(jax.random.fold_in(key, 11), device_count)
    return jax.vmap(single_device)(keys).reshape(device_count * ITEM_DEV, K).astype(jnp.int32)


def draw_neg_blocks(key, part):
    device_count = N_REGION * N_SHARD
    off_key, blk_key = jax.random.split(jax.random.fold_in(key, 23))
    region = (jnp.arange(device_count, dtype=jnp.int32) // N_SHARD)[:, None]
    offset = jax.random.randint(off_key, (device_count, NB), 1, N_REGION)
    local_block = jax.random.randint(blk_key, (device_count, NB), 0, BLK_DEV)
    return ((region + offset) % N_REGION * BLK_DEV + local_block).astype(jnp.int32)


def with_ends(result, rng, smallest, high):
    spot = [jax.random.randint(jax.random.fold_in(rng, axis), (), 0, length) for axis, length in enumerate(result.shape)]
    widest = result.shape.index(max(result.shape))
    beside = spot[:widest] + [(spot[widest] + 1) % result.shape[widest]] + spot[widest + 1:]
    return result.at[tuple(spot)].set(smallest).at[tuple(beside)].set(high)


def shard_levels(stream_key, extent, cuts, least, top_value):
    def one(dim, parts):
        draws = jax.random.uniform(jax.random.fold_in(jax.random.fold_in(stream_key, 6), dim), (parts,), jnp.float32, least / len(cuts), top_value / len(cuts))
        return jnp.repeat(jnp.exp(draws), extent[dim] // parts).reshape((-1,) + (1,) * (len(extent) - dim - 1))

    level = one(*cuts[0])
    for cut in cuts[1:]:
        level = level * one(*cut)
    return level


def noise(stream_key, dims, width, reach, cuts=(), kind=jnp.bfloat16):
    entries = jax.random.normal(stream_key, dims, jnp.float32) * width
    if len(cuts) > 0:
        entries = shard_levels(stream_key, dims, cuts, -0.22, 0.18) * entries
    return jnp.clip(entries, min=-reach, max=reach).astype(kind)


def setup_inputs(seed: int = 0) -> dict:
    seeds = jax.random.split(jax.random.key(seed), 13)
    return {
        "features": noise(seeds[0], (ITEMS, D), 1.0, 6.0, ((0, 256),)),
        "proj_weight": noise(seeds[1], (D, H), D ** -0.5, 0.1875),
        "proj_bias": noise(seeds[2], (H,), 0.5, 3.0, (), jnp.float32),
        "self_weight": noise(seeds[3], (D, H), D ** -0.5, 0.1875),
        "nbr_weight": noise(seeds[4], (H, H), H ** -0.5, 0.1875),
        "out_bias": noise(seeds[5], (H,), 0.5, 3.0, (), jnp.float32),
        "nbr_ids": draw_nbr_ids(jax.random.fold_in(seeds[12], 71), 0),
        "nbr_counts": with_ends(jax.random.randint(seeds[7], (ITEMS, K), 1, 33), jax.random.fold_in(seeds[7], 1), 1, 32).astype(jnp.int32),
        "live_slots": with_ends(jax.random.randint(seeds[8], (ITEMS // BLOCK,), 1, K + 1), jax.random.fold_in(seeds[8], 1), 1, K).astype(jnp.int32),
        "query_ids": with_ends(jax.random.randint(seeds[9], (QUERIES,), 0, ITEM_DEV), jax.random.fold_in(seeds[9], 1), 0, ITEM_DEV - 1).astype(jnp.int32),
        "positive_ids": with_ends(jax.random.randint(seeds[10], (QUERIES,), 0, ITEM_DEV), jax.random.fold_in(seeds[10], 1), 0, ITEM_DEV - 1).astype(jnp.int32),
        "neg_blocks": draw_neg_blocks(jax.random.fold_in(seeds[12], 71), 0),
    }


score_scale = 32.0
margin_value = 1.0
norm_eps = 1e-06

def reference(features, proj_weight, proj_bias, self_weight, nbr_weight, out_bias, nbr_ids, nbr_counts, live_slots, query_ids, positive_ids, neg_blocks):
    device_count = N_REGION * N_SHARD
    region_rows = N_SHARD * ITEM_DEV
    projected = jnp.maximum(jnp.dot(features, proj_weight, preferred_element_type=jnp.float32) + proj_bias, 0.0).astype(jnp.bfloat16)
    dev_feat = features.reshape(device_count, ITEM_DEV, D)
    dev_ids = nbr_ids.reshape(device_count, ITEM_DEV, K)
    dev_counts = nbr_counts.reshape(device_count, ITEM_DEV, K)
    dev_live = live_slots.reshape(device_count, BLK_DEV)

    def convolve(packed):
        device, feat, item_ids, counts, live = packed
        base = device // N_SHARD * region_rows
        rows = jnp.take(projected, (base + item_ids).astype(jnp.int32), axis=0)
        live_item = jnp.repeat(live, BLOCK, total_repeat_length=ITEM_DEV)
        slot_index = jnp.arange(K, dtype=jnp.int32)
        slot_weight = jnp.where(slot_index[None, :] < live_item[:, None], counts, 0).astype(jnp.float32)
        summed = jnp.einsum('ik,ikh->ih', slot_weight, rows.astype(jnp.float32))
        aggregate = (summed / lax.optimization_barrier(jnp.sum(slot_weight, axis=1, keepdims=True))).astype(jnp.bfloat16)
        activation = jnp.dot(feat, self_weight, preferred_element_type=jnp.float32) + jnp.dot(aggregate, nbr_weight, preferred_element_type=jnp.float32) + out_bias
        activation = jnp.maximum(activation, 0.0)
        scale_row = lax.rsqrt(lax.optimization_barrier(jnp.mean(activation * activation, axis=-1, keepdims=True)) + norm_eps)
        return (activation * scale_row).astype(jnp.bfloat16)
    devices_idx = jnp.arange(device_count, dtype=jnp.int32)
    embeds = lax.map(convolve, (devices_idx, dev_feat, dev_ids, dev_counts, dev_live))

    def score(packed):
        device, qids, pids, negs = packed
        mine = embeds[device]
        query_emb = jnp.take(mine, qids, axis=0)
        positive_emb = jnp.take(mine, pids, axis=0)
        positive_score = score_scale / H * lax.optimization_barrier(jnp.sum(query_emb.astype(jnp.float32) * positive_emb.astype(jnp.float32), axis=-1))
        shard_pos = device % N_SHARD

        def single_block(pool_block):
            holder = (pool_block // BLK_DEV * N_SHARD + shard_pos).astype(jnp.int32)
            first = (pool_block % BLK_DEV * BLOCK).astype(jnp.int32)
            block_rows = lax.dynamic_slice(embeds[holder], (first, jnp.int32(0)), (BLOCK, H))
            scores = score_scale / H * jnp.dot(query_emb, block_rows.T, preferred_element_type=jnp.float32)
            return lax.optimization_barrier(jnp.mean(jnp.maximum(scores - positive_score[:, None] + margin_value, 0.0), axis=-1))
        return jax.vmap(single_block)(negs).T
    hinge = lax.map(score, (devices_idx, query_ids.reshape(device_count, QD), positive_ids.reshape(device_count, QD), neg_blocks))
    return (embeds.reshape(ITEMS, H), hinge.reshape(QUERIES, NB))
```

```python
import jax
import jax.numpy as jnp
from jax import lax
from jax.sharding import PartitionSpec as P

score_scale = 32.0
margin_value = 1.0
norm_eps = 1e-06


def exclusive_counts(onehot, chunk):
    n, m = onehot.shape
    blocks = n // chunk
    oh = onehot.reshape(blocks, chunk, m)
    ii = lax.broadcasted_iota(jnp.int32, (chunk, chunk), 0)
    jj = lax.broadcasted_iota(jnp.int32, (chunk, chunk), 1)
    tri = (jj < ii).astype(jnp.bfloat16)
    within = jnp.einsum("ij,bjo->bio", tri, oh, preferred_element_type=jnp.float32)
    totals = jnp.sum(oh.astype(jnp.float32), axis=1)
    bi = lax.broadcasted_iota(jnp.int32, (blocks, blocks), 0)
    bj = lax.broadcasted_iota(jnp.int32, (blocks, blocks), 1)
    btri = (bj < bi).astype(jnp.float32)
    offsets = jnp.dot(btri, totals, precision=lax.Precision.HIGHEST)
    return (within + offsets[:, None, :]).reshape(n, m)


def body(
    features,
    proj_weight,
    proj_bias,
    self_weight,
    nbr_weight,
    out_bias,
    nbr_ids,
    nbr_counts,
    live_slots,
    query_ids,
    positive_ids,
    neg_blocks,
):
    item_dev = features.shape[0]
    hidden = proj_weight.shape[1]
    fanout = nbr_ids.shape[1]
    block_rows = item_dev // live_slots.shape[0]
    shards = lax.axis_size("shard")
    slots = item_dev * fanout
    capacity = max(2, 2 * slots // shards)

    projected = jnp.maximum(
        jnp.dot(features, proj_weight, preferred_element_type=jnp.float32) + proj_bias, 0.0
    ).astype(jnp.bfloat16)

    live_item = jnp.repeat(live_slots, block_rows, total_repeat_length=item_dev)
    slot_weight = jnp.where(
        jnp.arange(fanout, dtype=jnp.int32)[None, :] < live_item[:, None], nbr_counts, 0
    )
    weight_sum = jnp.sum(slot_weight.astype(jnp.float32), axis=1, keepdims=True)

    flat_ids = nbr_ids.reshape(-1)
    owners = flat_ids // item_dev
    local_row = flat_ids % item_dev
    owner_hot = owners[:, None] == jnp.arange(shards, dtype=jnp.int32)[None, :]
    counts = exclusive_counts(owner_hot.astype(jnp.bfloat16), 128)
    slot_rank = jnp.sum(jnp.where(owner_hot, counts, 0.0), axis=1).astype(jnp.int32)
    rank_hot = slot_rank[:, None] == jnp.arange(capacity, dtype=jnp.int32)[None, :]
    row_by_rank = jnp.where(rank_hot, local_row[:, None].astype(jnp.float32), 0.0)
    requests = jnp.dot(
        owner_hot.astype(jnp.bfloat16).T,
        row_by_rank.astype(jnp.bfloat16),
        preferred_element_type=jnp.float32,
    ).astype(jnp.int32)
    wanted = lax.all_to_all(requests, "shard", split_axis=0, concat_axis=0, tiled=True)
    pick = (
        wanted.reshape(-1)[:, None] == jnp.arange(item_dev, dtype=jnp.int32)[None, :]
    ).astype(jnp.bfloat16)
    outgoing = jnp.dot(pick, projected, preferred_element_type=jnp.float32).astype(jnp.bfloat16)
    outgoing = outgoing.reshape(shards, capacity, hidden)
    incoming = lax.all_to_all(outgoing, "shard", split_axis=0, concat_axis=0, tiled=True)

    column = (owners * capacity + slot_rank).reshape(item_dev, fanout)
    spread = jnp.where(
        column[:, :, None] == jnp.arange(shards * capacity, dtype=jnp.int32)[None, None, :],
        slot_weight[:, :, None].astype(jnp.float32),
        0.0,
    )
    mix = jnp.sum(spread, axis=1).astype(jnp.bfloat16)
    summed = jnp.dot(
        mix, incoming.reshape(shards * capacity, hidden), preferred_element_type=jnp.float32
    )
    aggregate = (summed / weight_sum).astype(jnp.bfloat16)
    activation = (
        jnp.dot(features, self_weight, preferred_element_type=jnp.float32)
        + jnp.dot(aggregate, nbr_weight, preferred_element_type=jnp.float32)
        + out_bias
    )
    activation = jnp.maximum(activation, 0.0)
    embedding = (
        activation * lax.rsqrt(jnp.mean(activation * activation, axis=-1, keepdims=True) + norm_eps)
    ).astype(jnp.bfloat16)

    items = jnp.arange(item_dev, dtype=jnp.int32)[None, :]
    query_pick = (query_ids[:, None] == items).astype(jnp.bfloat16)
    positive_pick = (positive_ids[:, None] == items).astype(jnp.bfloat16)
    query_emb = jnp.dot(query_pick, embedding, preferred_element_type=jnp.float32)
    positive_emb = jnp.dot(positive_pick, embedding, preferred_element_type=jnp.float32)
    positive_score = score_scale / hidden * jnp.sum(query_emb * positive_emb, axis=-1)
    neg_lists = neg_blocks[0]
    scores = (
        score_scale
        / hidden
        * jnp.dot(
            query_emb.astype(jnp.bfloat16),
            lax.all_gather(embedding, "region", axis=0, tiled=True).T,
            preferred_element_type=jnp.float32,
        )
    )
    hinge_all = jnp.maximum(scores - positive_score[:, None] + margin_value, 0.0)
    block_mean = jnp.mean(hinge_all.reshape(query_emb.shape[0], -1, block_rows), axis=-1)
    pool_ids = jnp.arange(block_mean.shape[1], dtype=jnp.int32)
    picked = jnp.where(
        neg_lists[None, :, None] == pool_ids[None, None, :], block_mean[:, None, :], 0.0
    )
    hinge_terms = jnp.sum(picked, axis=-1)
    return (embedding, hinge_terms)


def solution(mesh):
    in_specs = (
        P(("region", "shard"), None),
        P(),
        P(),
        P(),
        P(),
        P(),
        P(("region", "shard"), None),
        P(("region", "shard"), None),
        P(("region", "shard")),
        P(("region", "shard")),
        P(("region", "shard")),
        P(("region", "shard"), None),
    )
    out_specs = (P(("region", "shard"), None), P(("region", "shard"), None))
    return jax.shard_map(body, mesh=mesh, in_specs=in_specs, out_specs=out_specs, check_vma=False)
```

```python
import jax
import jax.numpy as jnp
from jax import lax
from jax.sharding import PartitionSpec as P

score_scale = 32.0
margin_value = 1.0
norm_eps = 1e-06


def exclusive_counts(onehot, chunk):
    n, m = onehot.shape
    blocks = n // chunk
    oh = onehot.reshape(blocks, chunk, m)
    ii = lax.broadcasted_iota(jnp.int32, (chunk, chunk), 0)
    jj = lax.broadcasted_iota(jnp.int32, (chunk, chunk), 1)
    tri = (jj < ii).astype(jnp.bfloat16)
    within = jnp.einsum("ij,bjo->bio", tri, oh, preferred_element_type=jnp.float32)
    totals = jnp.sum(oh.astype(jnp.float32), axis=1)
    bi = lax.broadcasted_iota(jnp.int32, (blocks, blocks), 0)
    bj = lax.broadcasted_iota(jnp.int32, (blocks, blocks), 1)
    btri = (bj < bi).astype(jnp.float32)
    offsets = jnp.dot(btri, totals, precision=lax.Precision.HIGHEST)
    return (within + offsets[:, None, :]).reshape(n, m)


def body(
    features,
    proj_weight,
    proj_bias,
    self_weight,
    nbr_weight,
    out_bias,
    nbr_ids,
    nbr_counts,
    live_slots,
    query_ids,
    positive_ids,
    neg_blocks,
):
    item_dev = features.shape[0]
    hidden = proj_weight.shape[1]
    fanout = nbr_ids.shape[1]
    block_rows = item_dev // live_slots.shape[0]
    shards = lax.axis_size("shard")
    slots = item_dev * fanout
    capacity = max(2, 2 * slots // shards)

    projected = jnp.maximum(
        jnp.dot(features, proj_weight, preferred_element_type=jnp.float32) + proj_bias, 0.0
    ).astype(jnp.bfloat16)

    live_item = jnp.repeat(live_slots, block_rows, total_repeat_length=item_dev)
    slot_weight = jnp.where(
        jnp.arange(fanout, dtype=jnp.int32)[None, :] < live_item[:, None], nbr_counts, 0
    )
    weight_sum = jnp.sum(slot_weight.astype(jnp.float32), axis=1, keepdims=True)

    flat_ids = nbr_ids.reshape(-1)
    owners = flat_ids // item_dev
    local_row = flat_ids % item_dev

    def exchange(server, value, rank, cap, table_of):
        server_hot = server[:, None] == jnp.arange(shards, dtype=jnp.int32)[None, :]
        rank_hot = rank[:, None] == jnp.arange(cap, dtype=jnp.int32)[None, :]
        lo = jnp.where(rank_hot, (value % item_dev)[:, None].astype(jnp.float32), 0.0)
        hi = jnp.where(rank_hot, (value // item_dev)[:, None].astype(jnp.float32), 0.0)
        both = jnp.dot(
            server_hot.astype(jnp.bfloat16).T,
            jnp.concatenate([lo, hi], axis=1).astype(jnp.bfloat16),
            preferred_element_type=jnp.float32,
        ).astype(jnp.int32)
        requests = both[:, cap:] * item_dev + both[:, :cap]
        wanted = lax.all_to_all(requests, "shard", split_axis=0, concat_axis=0, tiled=True)
        table, index = table_of(wanted.reshape(-1))
        pick = (index[:, None] == jnp.arange(table.shape[0], dtype=jnp.int32)[None, :]).astype(
            jnp.bfloat16
        )
        outgoing = jnp.dot(pick, table, preferred_element_type=jnp.float32).astype(jnp.bfloat16)
        outgoing = outgoing.reshape(shards, cap, hidden)
        incoming = lax.all_to_all(outgoing, "shard", split_axis=0, concat_axis=0, tiled=True)
        column = (server * cap + rank).reshape(item_dev, fanout)
        spread = jnp.where(
            column[:, :, None] == jnp.arange(shards * cap, dtype=jnp.int32)[None, None, :],
            slot_weight[:, :, None].astype(jnp.float32),
            0.0,
        )
        mix = jnp.sum(spread, axis=1).astype(jnp.bfloat16)
        return jnp.dot(
            mix, incoming.reshape(shards * cap, hidden), preferred_element_type=jnp.float32
        )

    def rank_within(group, groups):
        hot = group[:, None] == jnp.arange(groups, dtype=jnp.int32)[None, :]
        counts = exclusive_counts(hot.astype(jnp.bfloat16), 128)
        rank = jnp.sum(jnp.where(hot, counts, 0.0), axis=1).astype(jnp.int32)
        totals = jnp.sum(hot.astype(jnp.float32), axis=0)
        return rank, totals

    chips = shards // 2
    fast_cap = capacity * 3 // 4
    chip = owners // 2
    chip_rank, chip_totals = rank_within(chip, chips)
    crowded = jnp.max(chip_totals) > 2 * fast_cap
    any_crowded = lax.pmax(crowded.astype(jnp.int32), ("region", "shard"))

    def by_owner(_):
        rank, _totals = rank_within(owners, shards)
        return exchange(owners, local_row, rank, capacity, lambda w: (projected, w))

    def by_chip(_):
        core = lax.axis_index("shard") % 2
        pairs = [(i, i ^ 1) for i in range(shards)]
        sibling = lax.ppermute(projected, "shard", pairs)
        table = jnp.concatenate([projected, sibling], axis=0)

        def table_of(w):
            return table, ((w // item_dev) ^ core) * item_dev + w % item_dev

        server = chip * 2 + chip_rank % 2
        value = (owners % 2) * item_dev + local_row
        return exchange(server, value, chip_rank // 2, fast_cap, table_of)

    summed = lax.cond(any_crowded == 0, by_chip, by_owner, 0)
    aggregate = (summed / weight_sum).astype(jnp.bfloat16)
    activation = (
        jnp.dot(features, self_weight, preferred_element_type=jnp.float32)
        + jnp.dot(aggregate, nbr_weight, preferred_element_type=jnp.float32)
        + out_bias
    )
    activation = jnp.maximum(activation, 0.0)
    embedding = (
        activation * lax.rsqrt(jnp.mean(activation * activation, axis=-1, keepdims=True) + norm_eps)
    ).astype(jnp.bfloat16)

    items = jnp.arange(item_dev, dtype=jnp.int32)[None, :]
    query_pick = (query_ids[:, None] == items).astype(jnp.bfloat16)
    positive_pick = (positive_ids[:, None] == items).astype(jnp.bfloat16)
    query_emb = jnp.dot(query_pick, embedding, preferred_element_type=jnp.float32)
    positive_emb = jnp.dot(positive_pick, embedding, preferred_element_type=jnp.float32)
    positive_score = score_scale / hidden * jnp.sum(query_emb * positive_emb, axis=-1)
    neg_lists = neg_blocks[0]
    scores = (
        score_scale
        / hidden
        * jnp.dot(
            query_emb.astype(jnp.bfloat16),
            lax.all_gather(embedding, "region", axis=0, tiled=True).T,
            preferred_element_type=jnp.float32,
        )
    )
    hinge_all = jnp.maximum(scores - positive_score[:, None] + margin_value, 0.0)
    block_mean = jnp.mean(hinge_all.reshape(query_emb.shape[0], -1, block_rows), axis=-1)
    pool_ids = jnp.arange(block_mean.shape[1], dtype=jnp.int32)
    picked = jnp.where(
        neg_lists[None, :, None] == pool_ids[None, None, :], block_mean[:, None, :], 0.0
    )
    hinge_terms = jnp.sum(picked, axis=-1)
    return (embedding, hinge_terms)


def solution(mesh):
    in_specs = (
        P(("region", "shard"), None),
        P(),
        P(),
        P(),
        P(),
        P(),
        P(("region", "shard"), None),
        P(("region", "shard"), None),
        P(("region", "shard")),
        P(("region", "shard")),
        P(("region", "shard")),
        P(("region", "shard"), None),
    )
    out_specs = (P(("region", "shard"), None), P(("region", "shard"), None))
    return jax.shard_map(body, mesh=mesh, in_specs=in_specs, out_specs=out_specs, check_vma=False)
```

```python
import jax
import jax.numpy as jnp
from jax import lax
from jax.sharding import PartitionSpec as P

score_scale = 32.0
margin_value = 1.0
norm_eps = 1e-06


def exclusive_counts(onehot, chunk):
    n, m = onehot.shape
    blocks = n // chunk
    oh = onehot.reshape(blocks, chunk, m)
    ii = lax.broadcasted_iota(jnp.int32, (chunk, chunk), 0)
    jj = lax.broadcasted_iota(jnp.int32, (chunk, chunk), 1)
    tri = (jj < ii).astype(jnp.bfloat16)
    within = jnp.einsum("ij,bjo->bio", tri, oh, preferred_element_type=jnp.float32)
    totals = jnp.sum(oh.astype(jnp.float32), axis=1)
    bi = lax.broadcasted_iota(jnp.int32, (blocks, blocks), 0)
    bj = lax.broadcasted_iota(jnp.int32, (blocks, blocks), 1)
    btri = (bj < bi).astype(jnp.float32)
    offsets = jnp.dot(btri, totals, precision=lax.Precision.HIGHEST)
    return (within + offsets[:, None, :]).reshape(n, m)


def body(
    features,
    proj_weight,
    proj_bias,
    self_weight,
    nbr_weight,
    out_bias,
    nbr_ids,
    nbr_counts,
    live_slots,
    query_ids,
    positive_ids,
    neg_blocks,
):
    item_dev = features.shape[0]
    hidden = proj_weight.shape[1]
    fanout = nbr_ids.shape[1]
    block_rows = item_dev // live_slots.shape[0]
    shards = lax.axis_size("shard")
    slots = item_dev * fanout
    capacity = max(2, 2 * slots // shards)

    projected = jnp.maximum(
        jnp.dot(features, proj_weight, preferred_element_type=jnp.float32) + proj_bias, 0.0
    ).astype(jnp.bfloat16)

    live_item = jnp.repeat(live_slots, block_rows, total_repeat_length=item_dev)
    slot_weight = jnp.where(
        jnp.arange(fanout, dtype=jnp.int32)[None, :] < live_item[:, None], nbr_counts, 0
    )
    weight_sum = jnp.sum(slot_weight.astype(jnp.float32), axis=1, keepdims=True)

    flat_ids = nbr_ids.reshape(-1)
    owners = flat_ids // item_dev
    local_row = flat_ids % item_dev

    def make_requests(server, value, rank, cap):
        server_hot = server[:, None] == jnp.arange(shards, dtype=jnp.int32)[None, :]
        rank_hot = rank[:, None] == jnp.arange(cap, dtype=jnp.int32)[None, :]
        lo = jnp.where(rank_hot, (value % item_dev)[:, None].astype(jnp.float32), 0.0)
        hi = jnp.where(rank_hot, (value // item_dev)[:, None].astype(jnp.float32), 0.0)
        both = jnp.dot(
            server_hot.astype(jnp.bfloat16).T,
            jnp.concatenate([lo, hi], axis=1).astype(jnp.bfloat16),
            preferred_element_type=jnp.float32,
        ).astype(jnp.int32)
        return both[:, cap:] * item_dev + both[:, :cap]

    def serve(server, rank, cap, table, index):
        pick = (index[:, None] == jnp.arange(table.shape[0], dtype=jnp.int32)[None, :]).astype(
            jnp.bfloat16
        )
        outgoing = jnp.dot(pick, table, preferred_element_type=jnp.float32).astype(jnp.bfloat16)
        outgoing = outgoing.reshape(shards, cap, hidden)
        incoming = lax.all_to_all(outgoing, "shard", split_axis=0, concat_axis=0, tiled=True)
        column = (server * cap + rank).reshape(item_dev, fanout)
        spread = jnp.where(
            column[:, :, None] == jnp.arange(shards * cap, dtype=jnp.int32)[None, None, :],
            slot_weight[:, :, None].astype(jnp.float32),
            0.0,
        )
        mix = jnp.sum(spread, axis=1).astype(jnp.bfloat16)
        return jnp.dot(
            mix, incoming.reshape(shards * cap, hidden), preferred_element_type=jnp.float32
        )

    def rank_within(group, groups):
        hot = group[:, None] == jnp.arange(groups, dtype=jnp.int32)[None, :]
        counts = exclusive_counts(hot.astype(jnp.bfloat16), 128)
        rank = jnp.sum(jnp.where(hot, counts, 0.0), axis=1).astype(jnp.int32)
        totals = jnp.sum(hot.astype(jnp.float32), axis=0)
        return rank, totals

    chips = shards // 2
    fast_cap = capacity * 3 // 4
    chip = owners // 2
    chip_rank, chip_totals = rank_within(chip, chips)
    crowded = (jnp.max(chip_totals) > 2 * fast_cap).astype(jnp.int32)
    fast_server = chip * 2 + chip_rank % 2
    fast_rank = chip_rank // 2
    fast_requests = make_requests(
        fast_server, (owners % 2) * item_dev + local_row, fast_rank, fast_cap
    )
    flagged = jnp.concatenate(
        [fast_requests, jnp.broadcast_to(crowded, (shards, 1))], axis=1
    )
    received = lax.all_to_all(flagged, "shard", split_axis=0, concat_axis=0, tiled=True)
    region_crowded = jnp.max(received[:, fast_cap])
    core = lax.axis_index("shard") % 2
    pairs = [(i, i ^ 1) for i in range(shards)]
    sibling = lax.ppermute(projected, "shard", pairs)

    def by_owner(_):
        rank, _totals = rank_within(owners, shards)
        requests = make_requests(owners, local_row, rank, capacity)
        wanted = lax.all_to_all(requests, "shard", split_axis=0, concat_axis=0, tiled=True)
        return serve(owners, rank, capacity, projected, wanted.reshape(-1))

    def by_chip(_):
        wanted = received[:, :fast_cap].reshape(-1)
        index = ((wanted // item_dev) ^ core) * item_dev + wanted % item_dev
        table = jnp.concatenate([projected, sibling], axis=0)
        return serve(fast_server, fast_rank, fast_cap, table, index)

    summed = lax.cond(region_crowded == 0, by_chip, by_owner, 0)
    aggregate = (summed / weight_sum).astype(jnp.bfloat16)
    activation = (
        jnp.dot(features, self_weight, preferred_element_type=jnp.float32)
        + jnp.dot(aggregate, nbr_weight, preferred_element_type=jnp.float32)
        + out_bias
    )
    activation = jnp.maximum(activation, 0.0)
    embedding = (
        activation * lax.rsqrt(jnp.mean(activation * activation, axis=-1, keepdims=True) + norm_eps)
    ).astype(jnp.bfloat16)

    items = jnp.arange(item_dev, dtype=jnp.int32)[None, :]
    query_pick = (query_ids[:, None] == items).astype(jnp.bfloat16)
    positive_pick = (positive_ids[:, None] == items).astype(jnp.bfloat16)
    query_emb = jnp.dot(query_pick, embedding, preferred_element_type=jnp.float32)
    positive_emb = jnp.dot(positive_pick, embedding, preferred_element_type=jnp.float32)
    positive_score = score_scale / hidden * jnp.sum(query_emb * positive_emb, axis=-1)
    neg_lists = neg_blocks[0]
    scores = (
        score_scale
        / hidden
        * jnp.dot(
            query_emb.astype(jnp.bfloat16),
            lax.all_gather(embedding, "region", axis=0, tiled=True).T,
            preferred_element_type=jnp.float32,
        )
    )
    hinge_all = jnp.maximum(scores - positive_score[:, None] + margin_value, 0.0)
    block_mean = jnp.mean(hinge_all.reshape(query_emb.shape[0], -1, block_rows), axis=-1)
    pool_ids = jnp.arange(block_mean.shape[1], dtype=jnp.int32)
    picked = jnp.where(
        neg_lists[None, :, None] == pool_ids[None, None, :], block_mean[:, None, :], 0.0
    )
    hinge_terms = jnp.sum(picked, axis=-1)
    return (embedding, hinge_terms)


def solution(mesh):
    in_specs = (
        P(("region", "shard"), None),
        P(),
        P(),
        P(),
        P(),
        P(),
        P(("region", "shard"), None),
        P(("region", "shard"), None),
        P(("region", "shard")),
        P(("region", "shard")),
        P(("region", "shard")),
        P(("region", "shard"), None),
    )
    out_specs = (P(("region", "shard"), None), P(("region", "shard"), None))
    return jax.shard_map(body, mesh=mesh, in_specs=in_specs, out_specs=out_specs, check_vma=False)
```

```python
import jax
import jax.numpy as jnp
from jax import lax
from jax.sharding import PartitionSpec as P

score_scale = 32.0
margin_value = 1.0
norm_eps = 1e-06


def exclusive_counts(onehot, chunk):
    n, m = onehot.shape
    blocks = n // chunk
    oh = onehot.reshape(blocks, chunk, m)
    ii = lax.broadcasted_iota(jnp.int32, (chunk, chunk), 0)
    jj = lax.broadcasted_iota(jnp.int32, (chunk, chunk), 1)
    tri = (jj < ii).astype(jnp.bfloat16)
    within = jnp.einsum("ij,bjo->bio", tri, oh, preferred_element_type=jnp.float32)
    totals = jnp.sum(oh.astype(jnp.float32), axis=1)
    bi = lax.broadcasted_iota(jnp.int32, (blocks, blocks), 0)
    bj = lax.broadcasted_iota(jnp.int32, (blocks, blocks), 1)
    btri = (bj < bi).astype(jnp.float32)
    offsets = jnp.dot(btri, totals, precision=lax.Precision.HIGHEST)
    return (within + offsets[:, None, :]).reshape(n, m)


def body(
    features,
    proj_weight,
    proj_bias,
    self_weight,
    nbr_weight,
    out_bias,
    nbr_ids,
    nbr_counts,
    live_slots,
    query_ids,
    positive_ids,
    neg_blocks,
):
    item_dev = features.shape[0]
    hidden = proj_weight.shape[1]
    fanout = nbr_ids.shape[1]
    block_rows = item_dev // live_slots.shape[0]
    shards = lax.axis_size("shard")
    slots = item_dev * fanout
    capacity = max(2, 2 * slots // shards)

    projected = jnp.maximum(
        jnp.dot(features, proj_weight, preferred_element_type=jnp.float32) + proj_bias, 0.0
    ).astype(jnp.bfloat16)

    live_item = jnp.repeat(live_slots, block_rows, total_repeat_length=item_dev)
    slot_weight = jnp.where(
        jnp.arange(fanout, dtype=jnp.int32)[None, :] < live_item[:, None], nbr_counts, 0
    )
    weight_sum = jnp.sum(slot_weight.astype(jnp.float32), axis=1, keepdims=True)

    flat_ids = nbr_ids.reshape(-1)
    owners = flat_ids // item_dev
    local_row = flat_ids % item_dev

    def make_requests(server, value, rank, cap):
        server_hot = server[:, None] == jnp.arange(shards, dtype=jnp.int32)[None, :]
        rank_hot = rank[:, None] == jnp.arange(cap, dtype=jnp.int32)[None, :]
        lo = jnp.where(rank_hot, (value % item_dev)[:, None].astype(jnp.float32), 0.0)
        hi = jnp.where(rank_hot, (value // item_dev)[:, None].astype(jnp.float32), 0.0)
        both = jnp.dot(
            server_hot.astype(jnp.bfloat16).T,
            jnp.concatenate([lo, hi], axis=1).astype(jnp.bfloat16),
            preferred_element_type=jnp.float32,
        ).astype(jnp.int32)
        return both[:, cap:] * item_dev + both[:, :cap]

    def serve(server, rank, cap, table, index, valid):
        pick = (index[:, None] == jnp.arange(table.shape[0], dtype=jnp.int32)[None, :]).astype(
            jnp.bfloat16
        )
        outgoing = jnp.dot(pick, table, preferred_element_type=jnp.float32).astype(jnp.bfloat16)
        outgoing = outgoing.reshape(shards, cap, hidden)
        incoming = lax.all_to_all(outgoing, "shard", split_axis=0, concat_axis=0, tiled=True)
        column = (server * cap + rank).reshape(item_dev, fanout)
        weight = jnp.where(valid.reshape(item_dev, fanout), slot_weight, 0)
        spread = jnp.where(
            column[:, :, None] == jnp.arange(shards * cap, dtype=jnp.int32)[None, None, :],
            weight[:, :, None].astype(jnp.float32),
            0.0,
        )
        mix = jnp.sum(spread, axis=1).astype(jnp.bfloat16)
        return jnp.dot(
            mix, incoming.reshape(shards * cap, hidden), preferred_element_type=jnp.float32
        )

    def rank_within(group, groups):
        hot = group[:, None] == jnp.arange(groups, dtype=jnp.int32)[None, :]
        counts = exclusive_counts(hot.astype(jnp.bfloat16), 128)
        rank = jnp.sum(jnp.where(hot, counts, 0.0), axis=1).astype(jnp.int32)
        totals = jnp.sum(hot.astype(jnp.float32), axis=0)
        return rank, totals

    chips = shards // 2
    main_cap = capacity * 3 // 4
    spill_cap = capacity - main_cap
    chip = owners // 2
    chip_rank, chip_totals = rank_within(chip, chips)
    crowded = (jnp.max(chip_totals) > 2 * main_cap).astype(jnp.int32)
    server = chip * 2 + chip_rank % 2
    server_rank = chip_rank // 2
    value = (owners % 2) * item_dev + local_row
    requests = make_requests(server, value, server_rank, main_cap)
    flagged = jnp.concatenate([requests, jnp.broadcast_to(crowded, (shards, 1))], axis=1)
    received = lax.all_to_all(flagged, "shard", split_axis=0, concat_axis=0, tiled=True)
    region_crowded = jnp.max(received[:, main_cap])
    core = lax.axis_index("shard") % 2
    pairs = [(i, i ^ 1) for i in range(shards)]
    sibling = lax.ppermute(projected, "shard", pairs)
    table = jnp.concatenate([projected, sibling], axis=0)

    def table_index(wanted):
        return ((wanted // item_dev) ^ core) * item_dev + wanted % item_dev

    summed = serve(
        server,
        server_rank,
        main_cap,
        table,
        table_index(received[:, :main_cap].reshape(-1)),
        server_rank < main_cap,
    )

    def spill(_):
        spill_rank = server_rank - main_cap
        spill_requests = make_requests(server, value, spill_rank, spill_cap)
        wanted = lax.all_to_all(spill_requests, "shard", split_axis=0, concat_axis=0, tiled=True)
        return serve(
            server,
            spill_rank,
            spill_cap,
            table,
            table_index(wanted.reshape(-1)),
            spill_rank >= 0,
        )

    def no_spill(_):
        return jnp.zeros_like(summed)

    summed = summed + lax.cond(region_crowded == 0, no_spill, spill, 0)
    aggregate = (summed / weight_sum).astype(jnp.bfloat16)
    activation = (
        jnp.dot(features, self_weight, preferred_element_type=jnp.float32)
        + jnp.dot(aggregate, nbr_weight, preferred_element_type=jnp.float32)
        + out_bias
    )
    activation = jnp.maximum(activation, 0.0)
    embedding = (
        activation * lax.rsqrt(jnp.mean(activation * activation, axis=-1, keepdims=True) + norm_eps)
    ).astype(jnp.bfloat16)

    items = jnp.arange(item_dev, dtype=jnp.int32)[None, :]
    query_pick = (query_ids[:, None] == items).astype(jnp.bfloat16)
    positive_pick = (positive_ids[:, None] == items).astype(jnp.bfloat16)
    query_emb = jnp.dot(query_pick, embedding, preferred_element_type=jnp.float32)
    positive_emb = jnp.dot(positive_pick, embedding, preferred_element_type=jnp.float32)
    positive_score = score_scale / hidden * jnp.sum(query_emb * positive_emb, axis=-1)
    neg_lists = neg_blocks[0]
    scores = (
        score_scale
        / hidden
        * jnp.dot(
            query_emb.astype(jnp.bfloat16),
            lax.all_gather(embedding, "region", axis=0, tiled=True).T,
            preferred_element_type=jnp.float32,
        )
    )
    hinge_all = jnp.maximum(scores - positive_score[:, None] + margin_value, 0.0)
    block_mean = jnp.mean(hinge_all.reshape(query_emb.shape[0], -1, block_rows), axis=-1)
    pool_ids = jnp.arange(block_mean.shape[1], dtype=jnp.int32)
    picked = jnp.where(
        neg_lists[None, :, None] == pool_ids[None, None, :], block_mean[:, None, :], 0.0
    )
    hinge_terms = jnp.sum(picked, axis=-1)
    return (embedding, hinge_terms)


def solution(mesh):
    in_specs = (
        P(("region", "shard"), None),
        P(),
        P(),
        P(),
        P(),
        P(),
        P(("region", "shard"), None),
        P(("region", "shard"), None),
        P(("region", "shard")),
        P(("region", "shard")),
        P(("region", "shard")),
        P(("region", "shard"), None),
    )
    out_specs = (P(("region", "shard"), None), P(("region", "shard"), None))
    return jax.shard_map(body, mesh=mesh, in_specs=in_specs, out_specs=out_specs, check_vma=False)
```

```python
import jax
import jax.numpy as jnp
from jax import lax
from jax.sharding import PartitionSpec as P

score_scale = 32.0
margin_value = 1.0
norm_eps = 1e-06


def exclusive_counts(onehot, chunk):
    n, m = onehot.shape
    blocks = n // chunk
    oh = onehot.reshape(blocks, chunk, m)
    ii = lax.broadcasted_iota(jnp.int32, (chunk, chunk), 0)
    jj = lax.broadcasted_iota(jnp.int32, (chunk, chunk), 1)
    tri = (jj < ii).astype(jnp.bfloat16)
    within = jnp.einsum("ij,bjo->bio", tri, oh, preferred_element_type=jnp.float32)
    totals = jnp.sum(oh.astype(jnp.float32), axis=1)
    bi = lax.broadcasted_iota(jnp.int32, (blocks, blocks), 0)
    bj = lax.broadcasted_iota(jnp.int32, (blocks, blocks), 1)
    btri = (bj < bi).astype(jnp.float32)
    offsets = jnp.dot(btri, totals, precision=lax.Precision.HIGHEST)
    return (within + offsets[:, None, :]).reshape(n, m)


def body(
    features,
    proj_weight,
    proj_bias,
    self_weight,
    nbr_weight,
    out_bias,
    nbr_ids,
    nbr_counts,
    live_slots,
    query_ids,
    positive_ids,
    neg_blocks,
):
    item_dev = features.shape[0]
    hidden = proj_weight.shape[1]
    fanout = nbr_ids.shape[1]
    block_rows = item_dev // live_slots.shape[0]
    shards = lax.axis_size("shard")
    slots = item_dev * fanout
    capacity = max(2, 2 * slots // shards)

    projected = jnp.maximum(
        jnp.dot(features, proj_weight, preferred_element_type=jnp.float32) + proj_bias, 0.0
    ).astype(jnp.bfloat16)

    live_item = jnp.repeat(live_slots, block_rows, total_repeat_length=item_dev)
    slot_weight = jnp.where(
        jnp.arange(fanout, dtype=jnp.int32)[None, :] < live_item[:, None], nbr_counts, 0
    )
    weight_sum = jnp.sum(slot_weight.astype(jnp.float32), axis=1, keepdims=True)

    flat_ids = nbr_ids.reshape(-1)
    owners = flat_ids // item_dev
    local_row = flat_ids % item_dev

    def make_requests(server, value, rank, cap):
        server_hot = server[:, None] == jnp.arange(shards, dtype=jnp.int32)[None, :]
        rank_hot = rank[:, None] == jnp.arange(cap, dtype=jnp.int32)[None, :]
        lo = jnp.where(rank_hot, (value % item_dev)[:, None].astype(jnp.float32), 0.0)
        hi = jnp.where(rank_hot, (value // item_dev)[:, None].astype(jnp.float32), 0.0)
        both = jnp.dot(
            server_hot.astype(jnp.bfloat16).T,
            jnp.concatenate([lo, hi], axis=1).astype(jnp.bfloat16),
            preferred_element_type=jnp.float32,
        ).astype(jnp.int32)
        return both[:, cap:] * item_dev + both[:, :cap]

    def serve(server, rank, cap, table, index, valid):
        pick = (index[:, None] == jnp.arange(table.shape[0], dtype=jnp.int32)[None, :]).astype(
            jnp.bfloat16
        )
        outgoing = jnp.dot(pick, table, preferred_element_type=jnp.float32).astype(jnp.bfloat16)
        outgoing = outgoing.reshape(shards, cap, hidden)
        incoming = lax.all_to_all(outgoing, "shard", split_axis=0, concat_axis=0, tiled=True)
        column = (server * cap + rank).reshape(item_dev, fanout)
        weight = jnp.where(valid.reshape(item_dev, fanout), slot_weight, 0)
        spread = jnp.where(
            column[:, :, None] == jnp.arange(shards * cap, dtype=jnp.int32)[None, None, :],
            weight[:, :, None].astype(jnp.float32),
            0.0,
        )
        mix = jnp.sum(spread, axis=1).astype(jnp.bfloat16)
        return jnp.dot(
            mix, incoming.reshape(shards * cap, hidden), preferred_element_type=jnp.float32
        )

    def rank_within(group, groups):
        hot = group[:, None] == jnp.arange(groups, dtype=jnp.int32)[None, :]
        counts = exclusive_counts(hot.astype(jnp.bfloat16), 128)
        rank = jnp.sum(jnp.where(hot, counts, 0.0), axis=1).astype(jnp.int32)
        totals = jnp.sum(hot.astype(jnp.float32), axis=0)
        return rank, totals

    partner = shards // 4
    members = 4
    groups = shards // members
    main_cap = capacity * 5 // 8
    spill_cap = capacity - main_cap
    low = owners % 2
    high = (owners // partner) % 2
    group = (owners // (2 * partner)) * (partner // 2) + (owners % partner) // 2
    group_rank, group_totals = rank_within(group, groups)
    crowded = (jnp.max(group_totals) > members * main_cap).astype(jnp.int32)
    turn = group_rank % members
    group_base = (owners // (2 * partner)) * (2 * partner) + (owners % partner) // 2 * 2
    server = group_base + (turn // 2) * partner + turn % 2
    server_rank = group_rank // members
    value = (high * 2 + low) * item_dev + local_row
    requests = make_requests(server, value, server_rank, main_cap)
    flagged = jnp.concatenate([requests, jnp.broadcast_to(crowded, (shards, 1))], axis=1)
    received = lax.all_to_all(flagged, "shard", split_axis=0, concat_axis=0, tiled=True)
    region_crowded = jnp.max(received[:, main_cap])
    me = lax.axis_index("shard")
    my_code = ((me // partner) % 2) * 2 + me % 2
    sibling = lax.ppermute(projected, "shard", [(i, i ^ 1) for i in range(shards)])
    across = lax.ppermute(projected, "shard", [(i, i ^ partner) for i in range(shards)])
    across_sibling = lax.ppermute(across, "shard", [(i, i ^ 1) for i in range(shards)])
    table = jnp.concatenate([projected, sibling, across, across_sibling], axis=0)

    def table_index(wanted):
        return ((wanted // item_dev) ^ my_code) * item_dev + wanted % item_dev

    summed = serve(
        server,
        server_rank,
        main_cap,
        table,
        table_index(received[:, :main_cap].reshape(-1)),
        server_rank < main_cap,
    )

    def spill(_):
        spill_rank = server_rank - main_cap
        spill_requests = make_requests(server, value, spill_rank, spill_cap)
        wanted = lax.all_to_all(spill_requests, "shard", split_axis=0, concat_axis=0, tiled=True)
        return serve(
            server,
            spill_rank,
            spill_cap,
            table,
            table_index(wanted.reshape(-1)),
            spill_rank >= 0,
        )

    def no_spill(_):
        return jnp.zeros_like(summed)

    summed = summed + lax.cond(region_crowded == 0, no_spill, spill, 0)
    aggregate = (summed / weight_sum).astype(jnp.bfloat16)
    activation = (
        jnp.dot(features, self_weight, preferred_element_type=jnp.float32)
        + jnp.dot(aggregate, nbr_weight, preferred_element_type=jnp.float32)
        + out_bias
    )
    activation = jnp.maximum(activation, 0.0)
    embedding = (
        activation * lax.rsqrt(jnp.mean(activation * activation, axis=-1, keepdims=True) + norm_eps)
    ).astype(jnp.bfloat16)

    items = jnp.arange(item_dev, dtype=jnp.int32)[None, :]
    query_pick = (query_ids[:, None] == items).astype(jnp.bfloat16)
    positive_pick = (positive_ids[:, None] == items).astype(jnp.bfloat16)
    query_emb = jnp.dot(query_pick, embedding, preferred_element_type=jnp.float32)
    positive_emb = jnp.dot(positive_pick, embedding, preferred_element_type=jnp.float32)
    positive_score = score_scale / hidden * jnp.sum(query_emb * positive_emb, axis=-1)
    neg_lists = neg_blocks[0]
    scores = (
        score_scale
        / hidden
        * jnp.dot(
            query_emb.astype(jnp.bfloat16),
            lax.all_gather(embedding, "region", axis=0, tiled=True).T,
            preferred_element_type=jnp.float32,
        )
    )
    hinge_all = jnp.maximum(scores - positive_score[:, None] + margin_value, 0.0)
    block_mean = jnp.mean(hinge_all.reshape(query_emb.shape[0], -1, block_rows), axis=-1)
    pool_ids = jnp.arange(block_mean.shape[1], dtype=jnp.int32)
    picked = jnp.where(
        neg_lists[None, :, None] == pool_ids[None, None, :], block_mean[:, None, :], 0.0
    )
    hinge_terms = jnp.sum(picked, axis=-1)
    return (embedding, hinge_terms)


def solution(mesh):
    in_specs = (
        P(("region", "shard"), None),
        P(),
        P(),
        P(),
        P(),
        P(),
        P(("region", "shard"), None),
        P(("region", "shard"), None),
        P(("region", "shard")),
        P(("region", "shard")),
        P(("region", "shard")),
        P(("region", "shard"), None),
    )
    out_specs = (P(("region", "shard"), None), P(("region", "shard"), None))
    return jax.shard_map(body, mesh=mesh, in_specs=in_specs, out_specs=out_specs, check_vma=False)
```

```python
import jax
import jax.numpy as jnp
from jax import lax
from jax.sharding import PartitionSpec as P

score_scale = 32.0
margin_value = 1.0
norm_eps = 1e-06


def exclusive_counts(onehot, chunk):
    n, m = onehot.shape
    blocks = n // chunk
    oh = onehot.reshape(blocks, chunk, m)
    ii = lax.broadcasted_iota(jnp.int32, (chunk, chunk), 0)
    jj = lax.broadcasted_iota(jnp.int32, (chunk, chunk), 1)
    tri = (jj < ii).astype(jnp.bfloat16)
    within = jnp.einsum("ij,bjo->bio", tri, oh, preferred_element_type=jnp.float32)
    totals = jnp.sum(oh.astype(jnp.float32), axis=1)
    bi = lax.broadcasted_iota(jnp.int32, (blocks, blocks), 0)
    bj = lax.broadcasted_iota(jnp.int32, (blocks, blocks), 1)
    btri = (bj < bi).astype(jnp.float32)
    offsets = jnp.dot(btri, totals, precision=lax.Precision.HIGHEST)
    return (within + offsets[:, None, :]).reshape(n, m)


def body(
    features,
    proj_weight,
    proj_bias,
    self_weight,
    nbr_weight,
    out_bias,
    nbr_ids,
    nbr_counts,
    live_slots,
    query_ids,
    positive_ids,
    neg_blocks,
):
    item_dev = features.shape[0]
    hidden = proj_weight.shape[1]
    fanout = nbr_ids.shape[1]
    block_rows = item_dev // live_slots.shape[0]
    shards = lax.axis_size("shard")
    slots = item_dev * fanout
    capacity = max(2, 2 * slots // shards)

    projected = jnp.maximum(
        jnp.dot(features, proj_weight, preferred_element_type=jnp.float32) + proj_bias, 0.0
    ).astype(jnp.bfloat16)

    live_item = jnp.repeat(live_slots, block_rows, total_repeat_length=item_dev)
    slot_weight = jnp.where(
        jnp.arange(fanout, dtype=jnp.int32)[None, :] < live_item[:, None], nbr_counts, 0
    )
    weight_sum = jnp.sum(slot_weight.astype(jnp.float32), axis=1, keepdims=True)

    flat_ids = nbr_ids.reshape(-1)
    owners = flat_ids // item_dev
    local_row = flat_ids % item_dev

    def make_requests(server, value, rank, cap):
        server_hot = server[:, None] == jnp.arange(shards, dtype=jnp.int32)[None, :]
        rank_hot = rank[:, None] == jnp.arange(cap, dtype=jnp.int32)[None, :]
        lo = jnp.where(rank_hot, (value % item_dev)[:, None].astype(jnp.float32), 0.0)
        hi = jnp.where(rank_hot, (value // item_dev)[:, None].astype(jnp.float32), 0.0)
        both = jnp.dot(
            server_hot.astype(jnp.bfloat16).T,
            jnp.concatenate([lo, hi], axis=1).astype(jnp.bfloat16),
            preferred_element_type=jnp.float32,
        ).astype(jnp.int32)
        return both[:, cap:] * item_dev + both[:, :cap]

    def serve(server, rank, cap, table, index, valid):
        pick = (index[:, None] == jnp.arange(table.shape[0], dtype=jnp.int32)[None, :]).astype(
            jnp.bfloat16
        )
        outgoing = jnp.dot(pick, table, preferred_element_type=jnp.float32).astype(jnp.bfloat16)
        outgoing = outgoing.reshape(shards, cap, hidden)
        incoming = lax.all_to_all(outgoing, "shard", split_axis=0, concat_axis=0, tiled=True)
        column = (server * cap + rank).reshape(item_dev, fanout)
        weight = jnp.where(valid.reshape(item_dev, fanout), slot_weight, 0)
        spread = jnp.where(
            column[:, :, None] == jnp.arange(shards * cap, dtype=jnp.int32)[None, None, :],
            weight[:, :, None].astype(jnp.float32),
            0.0,
        )
        mix = jnp.sum(spread, axis=1).astype(jnp.bfloat16)
        return jnp.dot(
            mix, incoming.reshape(shards * cap, hidden), preferred_element_type=jnp.float32
        )

    def rank_within(group, groups):
        hot = group[:, None] == jnp.arange(groups, dtype=jnp.int32)[None, :]
        counts = exclusive_counts(hot.astype(jnp.bfloat16), 128)
        rank = jnp.sum(jnp.where(hot, counts, 0.0), axis=1).astype(jnp.int32)
        totals = jnp.sum(hot.astype(jnp.float32), axis=0)
        return rank, totals

    partner = shards // 4
    members = 4
    groups = shards // members
    main_cap = capacity * 5 // 8
    spill_cap = capacity - main_cap
    low = owners % 2
    high = (owners // partner) % 2
    group = (owners // (2 * partner)) * (partner // 2) + (owners % partner) // 2
    group_rank, group_totals = rank_within(group, groups)
    crowded = (jnp.max(group_totals) > members * main_cap).astype(jnp.int32)
    turn = group_rank % members
    group_base = (owners // (2 * partner)) * (2 * partner) + (owners % partner) // 2 * 2
    server = group_base + (turn // 2) * partner + turn % 2
    server_rank = group_rank // members
    value = (high * 2 + low) * item_dev + local_row
    requests = make_requests(server, value, server_rank, capacity)
    flagged = jnp.concatenate([requests, jnp.broadcast_to(crowded, (shards, 1))], axis=1)
    received = lax.all_to_all(flagged, "shard", split_axis=0, concat_axis=0, tiled=True)
    region_crowded = jnp.max(received[:, capacity])
    me = lax.axis_index("shard")
    my_code = ((me // partner) % 2) * 2 + me % 2
    across = lax.ppermute(projected, "shard", [(i, i ^ partner) for i in range(shards)])
    pair = jnp.concatenate([projected, across], axis=0)
    sibling = lax.ppermute(pair, "shard", [(i, i ^ 1) for i in range(shards)])
    table = jnp.concatenate(
        [projected, sibling[:item_dev], across, sibling[item_dev:]], axis=0
    )

    def table_index(wanted):
        return ((wanted // item_dev) ^ my_code) * item_dev + wanted % item_dev

    summed = serve(
        server,
        server_rank,
        main_cap,
        table,
        table_index(received[:, :main_cap].reshape(-1)),
        server_rank < main_cap,
    )

    def spill(_):
        spill_rank = server_rank - main_cap
        wanted = received[:, main_cap:capacity].reshape(-1)
        return serve(
            server, spill_rank, spill_cap, table, table_index(wanted), spill_rank >= 0
        )

    def no_spill(_):
        return jnp.zeros_like(summed)

    summed = summed + lax.cond(region_crowded == 0, no_spill, spill, 0)
    aggregate = (summed / weight_sum).astype(jnp.bfloat16)
    activation = (
        jnp.dot(features, self_weight, preferred_element_type=jnp.float32)
        + jnp.dot(aggregate, nbr_weight, preferred_element_type=jnp.float32)
        + out_bias
    )
    activation = jnp.maximum(activation, 0.0)
    embedding = (
        activation * lax.rsqrt(jnp.mean(activation * activation, axis=-1, keepdims=True) + norm_eps)
    ).astype(jnp.bfloat16)

    items = jnp.arange(item_dev, dtype=jnp.int32)[None, :]
    query_pick = (query_ids[:, None] == items).astype(jnp.bfloat16)
    positive_pick = (positive_ids[:, None] == items).astype(jnp.bfloat16)
    query_emb = jnp.dot(query_pick, embedding, preferred_element_type=jnp.float32)
    positive_emb = jnp.dot(positive_pick, embedding, preferred_element_type=jnp.float32)
    queries = query_emb.shape[0]
    pairs_rows = jnp.concatenate([query_emb, positive_emb], axis=0).astype(jnp.bfloat16)
    everyone = lax.all_gather(pairs_rows, "region", axis=0, tiled=False)
    their_queries = everyone[:, :queries]
    their_positives = everyone[:, queries:]
    positive_score = (
        score_scale
        / hidden
        * jnp.sum(
            their_queries.astype(jnp.float32) * their_positives.astype(jnp.float32), axis=-1
        )
    )
    scores = (
        score_scale
        / hidden
        * jnp.einsum(
            "rqh,ih->rqi", their_queries, embedding, preferred_element_type=jnp.float32
        )
    )
    hinge_all = jnp.maximum(scores - positive_score[:, :, None] + margin_value, 0.0)
    regions = everyone.shape[0]
    local_mean = jnp.mean(hinge_all.reshape(regions, queries, -1, block_rows), axis=-1)
    returned = lax.all_to_all(local_mean, "region", split_axis=0, concat_axis=0, tiled=True)
    block_mean = returned.transpose(1, 0, 2).reshape(queries, -1)
    neg_lists = neg_blocks[0]
    pool_ids = jnp.arange(block_mean.shape[1], dtype=jnp.int32)
    picked = jnp.where(
        neg_lists[None, :, None] == pool_ids[None, None, :], block_mean[:, None, :], 0.0
    )
    hinge_terms = jnp.sum(picked, axis=-1)
    return (embedding, hinge_terms)


def solution(mesh):
    in_specs = (
        P(("region", "shard"), None),
        P(),
        P(),
        P(),
        P(),
        P(),
        P(("region", "shard"), None),
        P(("region", "shard"), None),
        P(("region", "shard")),
        P(("region", "shard")),
        P(("region", "shard")),
        P(("region", "shard"), None),
    )
    out_specs = (P(("region", "shard"), None), P(("region", "shard"), None))
    return jax.shard_map(body, mesh=mesh, in_specs=in_specs, out_specs=out_specs, check_vma=False)
```

```python
import jax
import jax.numpy as jnp
from jax import lax
from jax.sharding import PartitionSpec as P

score_scale = 32.0
margin_value = 1.0
norm_eps = 1e-06


def exclusive_counts(onehot, chunk):
    n, m = onehot.shape
    blocks = n // chunk
    oh = onehot.reshape(blocks, chunk, m)
    ii = lax.broadcasted_iota(jnp.int32, (chunk, chunk), 0)
    jj = lax.broadcasted_iota(jnp.int32, (chunk, chunk), 1)
    tri = (jj < ii).astype(jnp.bfloat16)
    within = jnp.einsum("ij,bjo->bio", tri, oh, preferred_element_type=jnp.float32)
    totals = jnp.sum(oh.astype(jnp.float32), axis=1)
    bi = lax.broadcasted_iota(jnp.int32, (blocks, blocks), 0)
    bj = lax.broadcasted_iota(jnp.int32, (blocks, blocks), 1)
    btri = (bj < bi).astype(jnp.float32)
    offsets = jnp.dot(btri, totals, precision=lax.Precision.HIGHEST)
    return (within + offsets[:, None, :]).reshape(n, m)


def body(
    features,
    proj_weight,
    proj_bias,
    self_weight,
    nbr_weight,
    out_bias,
    nbr_ids,
    nbr_counts,
    live_slots,
    query_ids,
    positive_ids,
    neg_blocks,
):
    item_dev = features.shape[0]
    hidden = proj_weight.shape[1]
    fanout = nbr_ids.shape[1]
    block_rows = item_dev // live_slots.shape[0]
    shards = lax.axis_size("shard")
    slots = item_dev * fanout
    capacity = max(2, 2 * slots // shards)

    projected = jnp.maximum(
        jnp.dot(features, proj_weight, preferred_element_type=jnp.float32) + proj_bias, 0.0
    ).astype(jnp.bfloat16)

    live_item = jnp.repeat(live_slots, block_rows, total_repeat_length=item_dev)
    slot_weight = jnp.where(
        jnp.arange(fanout, dtype=jnp.int32)[None, :] < live_item[:, None], nbr_counts, 0
    )
    weight_sum = jnp.sum(slot_weight.astype(jnp.float32), axis=1, keepdims=True)

    flat_ids = nbr_ids.reshape(-1)
    owners = flat_ids // item_dev
    local_row = flat_ids % item_dev

    def make_requests(server, value, rank, cap):
        server_hot = server[:, None] == jnp.arange(shards, dtype=jnp.int32)[None, :]
        rank_hot = rank[:, None] == jnp.arange(cap, dtype=jnp.int32)[None, :]
        lo = jnp.where(rank_hot, (value % item_dev)[:, None].astype(jnp.float32), 0.0)
        hi = jnp.where(rank_hot, (value // item_dev)[:, None].astype(jnp.float32), 0.0)
        both = jnp.dot(
            server_hot.astype(jnp.bfloat16).T,
            jnp.concatenate([lo, hi], axis=1).astype(jnp.bfloat16),
            preferred_element_type=jnp.float32,
        ).astype(jnp.int32)
        return both[:, cap:] * item_dev + both[:, :cap]

    def serve(server, rank, cap, table, index, valid):
        pick = (index[:, None] == jnp.arange(table.shape[0], dtype=jnp.int32)[None, :]).astype(
            jnp.bfloat16
        )
        outgoing = jnp.dot(pick, table, preferred_element_type=jnp.float32).astype(jnp.bfloat16)
        outgoing = outgoing.reshape(shards, cap, hidden)
        incoming = lax.all_to_all(outgoing, "shard", split_axis=0, concat_axis=0, tiled=True)
        column = (server * cap + rank).reshape(item_dev, fanout)
        weight = jnp.where(valid.reshape(item_dev, fanout), slot_weight, 0)
        spread = jnp.where(
            column[:, :, None] == jnp.arange(shards * cap, dtype=jnp.int32)[None, None, :],
            weight[:, :, None].astype(jnp.float32),
            0.0,
        )
        mix = jnp.sum(spread, axis=1).astype(jnp.bfloat16)
        return jnp.dot(
            mix, incoming.reshape(shards * cap, hidden), preferred_element_type=jnp.float32
        )

    def rank_within(group, groups):
        hot = group[:, None] == jnp.arange(groups, dtype=jnp.int32)[None, :]
        counts = exclusive_counts(hot.astype(jnp.bfloat16), 128)
        rank = jnp.sum(jnp.where(hot, counts, 0.0), axis=1).astype(jnp.int32)
        totals = jnp.sum(hot.astype(jnp.float32), axis=0)
        return rank, totals

    partner = shards // 4
    members = 4
    groups = shards // members
    main_cap = capacity * 5 // 8
    spill_cap = capacity - main_cap
    low = owners % 2
    high = (owners // partner) % 2
    group = (owners // (2 * partner)) * (partner // 2) + (owners % partner) // 2
    group_rank, group_totals = rank_within(group, groups)
    crowded = (jnp.max(group_totals) > members * main_cap).astype(jnp.int32)
    turn = group_rank % members
    group_base = (owners // (2 * partner)) * (2 * partner) + (owners % partner) // 2 * 2
    server = group_base + (turn // 2) * partner + turn % 2
    server_rank = group_rank // members
    value = (high * 2 + low) * item_dev + local_row
    requests = make_requests(server, value, server_rank, capacity)
    flagged = jnp.concatenate([requests, jnp.broadcast_to(crowded, (shards, 1))], axis=1)
    received = lax.all_to_all(flagged, "shard", split_axis=0, concat_axis=0, tiled=True)
    region_crowded = jnp.max(received[:, capacity])
    me = lax.axis_index("shard")
    my_code = ((me // partner) % 2) * 2 + me % 2
    sibling = lax.ppermute(projected, "shard", [(i, i ^ 1) for i in range(shards)])
    across = lax.ppermute(projected, "shard", [(i, i ^ partner) for i in range(shards)])
    across_sibling = lax.ppermute(across, "shard", [(i, i ^ 1) for i in range(shards)])
    table = jnp.concatenate([projected, sibling, across, across_sibling], axis=0)

    def table_index(wanted):
        return ((wanted // item_dev) ^ my_code) * item_dev + wanted % item_dev

    summed = serve(
        server,
        server_rank,
        main_cap,
        table,
        table_index(received[:, :main_cap].reshape(-1)),
        server_rank < main_cap,
    )

    def spill(_):
        spill_rank = server_rank - main_cap
        wanted = received[:, main_cap:capacity].reshape(-1)
        return serve(
            server, spill_rank, spill_cap, table, table_index(wanted), spill_rank >= 0
        )

    def no_spill(_):
        return jnp.zeros_like(summed)

    summed = summed + lax.cond(region_crowded == 0, no_spill, spill, 0)
    aggregate = (summed / weight_sum).astype(jnp.bfloat16)
    activation = (
        jnp.dot(features, self_weight, preferred_element_type=jnp.float32)
        + jnp.dot(aggregate, nbr_weight, preferred_element_type=jnp.float32)
        + out_bias
    )
    activation = jnp.maximum(activation, 0.0)
    embedding = (
        activation * lax.rsqrt(jnp.mean(activation * activation, axis=-1, keepdims=True) + norm_eps)
    ).astype(jnp.bfloat16)

    items = jnp.arange(item_dev, dtype=jnp.int32)[None, :]
    query_pick = (query_ids[:, None] == items).astype(jnp.bfloat16)
    positive_pick = (positive_ids[:, None] == items).astype(jnp.bfloat16)
    query_emb = jnp.dot(query_pick, embedding, preferred_element_type=jnp.float32)
    positive_emb = jnp.dot(positive_pick, embedding, preferred_element_type=jnp.float32)
    positive_score = score_scale / hidden * jnp.sum(query_emb * positive_emb, axis=-1)
    neg_lists = neg_blocks[0]
    scores = (
        score_scale
        / hidden
        * jnp.dot(
            query_emb.astype(jnp.bfloat16),
            lax.all_gather(embedding, "region", axis=0, tiled=True).T,
            preferred_element_type=jnp.float32,
        )
    )
    hinge_all = jnp.maximum(scores - positive_score[:, None] + margin_value, 0.0)
    block_mean = jnp.mean(hinge_all.reshape(query_emb.shape[0], -1, block_rows), axis=-1)
    pool_ids = jnp.arange(block_mean.shape[1], dtype=jnp.int32)
    picked = jnp.where(
        neg_lists[None, :, None] == pool_ids[None, None, :], block_mean[:, None, :], 0.0
    )
    hinge_terms = jnp.sum(picked, axis=-1)
    return (embedding, hinge_terms)


def solution(mesh):
    in_specs = (
        P(("region", "shard"), None),
        P(),
        P(),
        P(),
        P(),
        P(),
        P(("region", "shard"), None),
        P(("region", "shard"), None),
        P(("region", "shard")),
        P(("region", "shard")),
        P(("region", "shard")),
        P(("region", "shard"), None),
    )
    out_specs = (P(("region", "shard"), None), P(("region", "shard"), None))
    return jax.shard_map(body, mesh=mesh, in_specs=in_specs, out_specs=out_specs, check_vma=False)
```

```python
import jax
import jax.numpy as jnp
from jax import lax
from jax.sharding import PartitionSpec as P

score_scale = 32.0
margin_value = 1.0
norm_eps = 1e-06


def exclusive_counts(onehot, chunk):
    n, m = onehot.shape
    blocks = n // chunk
    oh = onehot.reshape(blocks, chunk, m)
    ii = lax.broadcasted_iota(jnp.int32, (chunk, chunk), 0)
    jj = lax.broadcasted_iota(jnp.int32, (chunk, chunk), 1)
    tri = (jj < ii).astype(jnp.bfloat16)
    within = jnp.einsum("ij,bjo->bio", tri, oh, preferred_element_type=jnp.float32)
    totals = jnp.sum(oh.astype(jnp.float32), axis=1)
    bi = lax.broadcasted_iota(jnp.int32, (blocks, blocks), 0)
    bj = lax.broadcasted_iota(jnp.int32, (blocks, blocks), 1)
    btri = (bj < bi).astype(jnp.float32)
    offsets = jnp.dot(btri, totals, precision=lax.Precision.HIGHEST)
    return (within + offsets[:, None, :]).reshape(n, m)


def body(
    features,
    proj_weight,
    proj_bias,
    self_weight,
    nbr_weight,
    out_bias,
    nbr_ids,
    nbr_counts,
    live_slots,
    query_ids,
    positive_ids,
    neg_blocks,
):
    item_dev = features.shape[0]
    hidden = proj_weight.shape[1]
    fanout = nbr_ids.shape[1]
    block_rows = item_dev // live_slots.shape[0]
    shards = lax.axis_size("shard")
    slots = item_dev * fanout
    capacity = max(2, 2 * slots // shards)

    projected = jnp.maximum(
        jnp.dot(features, proj_weight, preferred_element_type=jnp.float32) + proj_bias, 0.0
    ).astype(jnp.bfloat16)

    live_item = jnp.repeat(live_slots, block_rows, total_repeat_length=item_dev)
    slot_weight = jnp.where(
        jnp.arange(fanout, dtype=jnp.int32)[None, :] < live_item[:, None], nbr_counts, 0
    )
    weight_sum = jnp.sum(slot_weight.astype(jnp.float32), axis=1, keepdims=True)

    flat_ids = nbr_ids.reshape(-1)
    owners = flat_ids // item_dev
    local_row = flat_ids % item_dev

    def make_requests(server, value, rank, cap):
        server_hot = server[:, None] == jnp.arange(shards, dtype=jnp.int32)[None, :]
        rank_hot = rank[:, None] == jnp.arange(cap, dtype=jnp.int32)[None, :]
        lo = jnp.where(rank_hot, (value % item_dev)[:, None].astype(jnp.float32), 0.0)
        hi = jnp.where(rank_hot, (value // item_dev)[:, None].astype(jnp.float32), 0.0)
        both = jnp.dot(
            server_hot.astype(jnp.bfloat16).T,
            jnp.concatenate([lo, hi], axis=1).astype(jnp.bfloat16),
            preferred_element_type=jnp.float32,
        ).astype(jnp.int32)
        return both[:, cap:] * item_dev + both[:, :cap]

    def serve(server, rank, cap, table, index, valid):
        pick = (index[:, None] == jnp.arange(table.shape[0], dtype=jnp.int32)[None, :]).astype(
            jnp.bfloat16
        )
        outgoing = jnp.dot(pick, table, preferred_element_type=jnp.float32).astype(jnp.bfloat16)
        outgoing = outgoing.reshape(shards, cap, hidden)
        incoming = lax.all_to_all(outgoing, "shard", split_axis=0, concat_axis=0, tiled=True)
        column = (server * cap + rank).reshape(item_dev, fanout)
        weight = jnp.where(valid.reshape(item_dev, fanout), slot_weight, 0)
        spread = jnp.where(
            column[:, :, None] == jnp.arange(shards * cap, dtype=jnp.int32)[None, None, :],
            weight[:, :, None].astype(jnp.float32),
            0.0,
        )
        mix = jnp.sum(spread, axis=1).astype(jnp.bfloat16)
        return jnp.dot(
            mix, incoming.reshape(shards * cap, hidden), preferred_element_type=jnp.float32
        )

    def rank_within(group, groups):
        hot = group[:, None] == jnp.arange(groups, dtype=jnp.int32)[None, :]
        counts = exclusive_counts(hot.astype(jnp.bfloat16), 128)
        rank = jnp.sum(jnp.where(hot, counts, 0.0), axis=1).astype(jnp.int32)
        totals = jnp.sum(hot.astype(jnp.float32), axis=0)
        return rank, totals

    partner = shards // 4
    members = 4
    groups = shards // members
    main_cap = capacity * 5 // 8
    spill_cap = capacity - main_cap
    low = owners % 2
    high = (owners // partner) % 2
    group = (owners // (2 * partner)) * (partner // 2) + (owners % partner) // 2
    group_rank, group_totals = rank_within(group, groups)
    crowded = (jnp.max(group_totals) > members * main_cap).astype(jnp.int32)
    turn = group_rank % members
    group_base = (owners // (2 * partner)) * (2 * partner) + (owners % partner) // 2 * 2
    server = group_base + (turn // 2) * partner + turn % 2
    server_rank = group_rank // members
    value = (high * 2 + low) * item_dev + local_row
    requests = make_requests(server, value, server_rank, capacity)
    flagged = jnp.concatenate([requests, jnp.broadcast_to(crowded, (shards, 1))], axis=1)
    received = lax.all_to_all(flagged, "shard", split_axis=0, concat_axis=0, tiled=True)
    region_crowded = jnp.max(received[:, capacity])
    me = lax.axis_index("shard")
    my_code = ((me // partner) % 2) * 2 + me % 2
    sibling = lax.ppermute(projected, "shard", [(i, i ^ 1) for i in range(shards)])
    across = lax.ppermute(projected, "shard", [(i, i ^ partner) for i in range(shards)])
    across_sibling = lax.ppermute(across, "shard", [(i, i ^ 1) for i in range(shards)])
    table = jnp.concatenate([projected, sibling, across, across_sibling], axis=0)

    def table_index(wanted):
        return ((wanted // item_dev) ^ my_code) * item_dev + wanted % item_dev

    summed = serve(
        server,
        server_rank,
        main_cap,
        table,
        table_index(received[:, :main_cap].reshape(-1)),
        server_rank < main_cap,
    )

    def spill(_):
        spill_rank = server_rank - main_cap
        wanted = received[:, main_cap:capacity].reshape(-1)
        return serve(
            server, spill_rank, spill_cap, table, table_index(wanted), spill_rank >= 0
        )

    def no_spill(_):
        return jnp.zeros_like(summed)

    summed = summed + lax.cond(region_crowded == 0, no_spill, spill, 0)
    aggregate = (summed / weight_sum).astype(jnp.bfloat16)
    activation = (
        jnp.dot(features, self_weight, preferred_element_type=jnp.float32)
        + jnp.dot(aggregate, nbr_weight, preferred_element_type=jnp.float32)
        + out_bias
    )
    activation = jnp.maximum(activation, 0.0)
    embedding = (
        activation * lax.rsqrt(jnp.mean(activation * activation, axis=-1, keepdims=True) + norm_eps)
    ).astype(jnp.bfloat16)

    items = jnp.arange(item_dev, dtype=jnp.int32)[None, :]
    query_pick = (query_ids[:, None] == items).astype(jnp.bfloat16)
    positive_pick = (positive_ids[:, None] == items).astype(jnp.bfloat16)
    query_emb = jnp.dot(query_pick, embedding, preferred_element_type=jnp.float32)
    positive_emb = jnp.dot(positive_pick, embedding, preferred_element_type=jnp.float32)
    positive_score = score_scale / hidden * jnp.sum(query_emb * positive_emb, axis=-1)
    neg_lists = neg_blocks[0]
    scores = (
        score_scale
        / hidden
        * jnp.dot(
            query_emb.astype(jnp.bfloat16),
            lax.all_to_all(
                jnp.tile(embedding, (lax.axis_size("region"), 1)),
                "region",
                split_axis=0,
                concat_axis=0,
                tiled=True,
            ).T,
            preferred_element_type=jnp.float32,
        )
    )
    hinge_all = jnp.maximum(scores - positive_score[:, None] + margin_value, 0.0)
    block_mean = jnp.mean(hinge_all.reshape(query_emb.shape[0], -1, block_rows), axis=-1)
    pool_ids = jnp.arange(block_mean.shape[1], dtype=jnp.int32)
    picked = jnp.where(
        neg_lists[None, :, None] == pool_ids[None, None, :], block_mean[:, None, :], 0.0
    )
    hinge_terms = jnp.sum(picked, axis=-1)
    return (embedding, hinge_terms)


def solution(mesh):
    in_specs = (
        P(("region", "shard"), None),
        P(),
        P(),
        P(),
        P(),
        P(),
        P(("region", "shard"), None),
        P(("region", "shard"), None),
        P(("region", "shard")),
        P(("region", "shard")),
        P(("region", "shard")),
        P(("region", "shard"), None),
    )
    out_specs = (P(("region", "shard"), None), P(("region", "shard"), None))
    return jax.shard_map(body, mesh=mesh, in_specs=in_specs, out_specs=out_specs, check_vma=False)
```

```python
import jax
import jax.numpy as jnp
from jax import lax
from jax.sharding import PartitionSpec as P

score_scale = 32.0
margin_value = 1.0
norm_eps = 1e-06


def exclusive_counts(onehot, chunk):
    n, m = onehot.shape
    blocks = n // chunk
    oh = onehot.reshape(blocks, chunk, m)
    ii = lax.broadcasted_iota(jnp.int32, (chunk, chunk), 0)
    jj = lax.broadcasted_iota(jnp.int32, (chunk, chunk), 1)
    tri = (jj < ii).astype(jnp.bfloat16)
    within = jnp.einsum("ij,bjo->bio", tri, oh, preferred_element_type=jnp.float32)
    totals = jnp.sum(oh.astype(jnp.float32), axis=1)
    bi = lax.broadcasted_iota(jnp.int32, (blocks, blocks), 0)
    bj = lax.broadcasted_iota(jnp.int32, (blocks, blocks), 1)
    btri = (bj < bi).astype(jnp.float32)
    offsets = jnp.dot(btri, totals, precision=lax.Precision.HIGHEST)
    return (within + offsets[:, None, :]).reshape(n, m)


def body(
    features,
    proj_weight,
    proj_bias,
    self_weight,
    nbr_weight,
    out_bias,
    nbr_ids,
    nbr_counts,
    live_slots,
    query_ids,
    positive_ids,
    neg_blocks,
):
    item_dev = features.shape[0]
    hidden = proj_weight.shape[1]
    fanout = nbr_ids.shape[1]
    block_rows = item_dev // live_slots.shape[0]
    shards = lax.axis_size("shard")
    slots = item_dev * fanout
    capacity = max(2, 2 * slots // shards)

    projected = jnp.maximum(
        jnp.dot(features, proj_weight, preferred_element_type=jnp.float32) + proj_bias, 0.0
    ).astype(jnp.bfloat16)

    live_item = jnp.repeat(live_slots, block_rows, total_repeat_length=item_dev)
    slot_weight = jnp.where(
        jnp.arange(fanout, dtype=jnp.int32)[None, :] < live_item[:, None], nbr_counts, 0
    )
    weight_sum = jnp.sum(slot_weight.astype(jnp.float32), axis=1, keepdims=True)

    flat_ids = nbr_ids.reshape(-1)
    owners = flat_ids // item_dev
    local_row = flat_ids % item_dev

    def make_requests(server, value, rank, cap):
        server_hot = server[:, None] == jnp.arange(shards, dtype=jnp.int32)[None, :]
        rank_hot = rank[:, None] == jnp.arange(cap, dtype=jnp.int32)[None, :]
        lo = jnp.where(rank_hot, (value % item_dev)[:, None].astype(jnp.float32), 0.0)
        hi = jnp.where(rank_hot, (value // item_dev)[:, None].astype(jnp.float32), 0.0)
        both = jnp.dot(
            server_hot.astype(jnp.bfloat16).T,
            jnp.concatenate([lo, hi], axis=1).astype(jnp.bfloat16),
            preferred_element_type=jnp.float32,
        ).astype(jnp.int32)
        return both[:, cap:] * item_dev + both[:, :cap]

    def serve(server, rank, cap, table, index, valid):
        pick = (index[:, None] == jnp.arange(table.shape[0], dtype=jnp.int32)[None, :]).astype(
            jnp.bfloat16
        )
        outgoing = jnp.dot(pick, table, preferred_element_type=jnp.float32).astype(jnp.bfloat16)
        outgoing = outgoing.reshape(shards, cap, hidden)
        incoming = lax.all_to_all(outgoing, "shard", split_axis=0, concat_axis=0, tiled=True)
        column = (server * cap + rank).reshape(item_dev, fanout)
        weight = jnp.where(valid.reshape(item_dev, fanout), slot_weight, 0)
        spread = jnp.where(
            column[:, :, None] == jnp.arange(shards * cap, dtype=jnp.int32)[None, None, :],
            weight[:, :, None].astype(jnp.float32),
            0.0,
        )
        mix = jnp.sum(spread, axis=1).astype(jnp.bfloat16)
        return jnp.dot(
            mix, incoming.reshape(shards * cap, hidden), preferred_element_type=jnp.float32
        )

    def rank_within(group, groups):
        hot = group[:, None] == jnp.arange(groups, dtype=jnp.int32)[None, :]
        counts = exclusive_counts(hot.astype(jnp.bfloat16), 128)
        rank = jnp.sum(jnp.where(hot, counts, 0.0), axis=1).astype(jnp.int32)
        totals = jnp.sum(hot.astype(jnp.float32), axis=0)
        return rank, totals

    partner = shards // 4
    members = 4
    groups = shards // members
    main_cap = capacity * 5 // 8
    spill_cap = capacity - main_cap
    low = owners % 2
    high = (owners // partner) % 2
    group = (owners // (2 * partner)) * (partner // 2) + (owners % partner) // 2
    group_rank, group_totals = rank_within(group, groups)
    crowded = (jnp.max(group_totals) > members * main_cap).astype(jnp.int32)
    turn = group_rank % members
    group_base = (owners // (2 * partner)) * (2 * partner) + (owners % partner) // 2 * 2
    server = group_base + (turn // 2) * partner + turn % 2
    server_rank = group_rank // members
    value = (high * 2 + low) * item_dev + local_row
    requests = make_requests(server, value, server_rank, capacity)
    flagged = jnp.concatenate([requests, jnp.broadcast_to(crowded, (shards, 1))], axis=1)
    received = lax.all_to_all(flagged, "shard", split_axis=0, concat_axis=0, tiled=True)
    region_crowded = jnp.max(received[:, capacity])
    me = lax.axis_index("shard")
    my_code = ((me // partner) % 2) * 2 + me % 2
    sibling = lax.ppermute(projected, "shard", [(i, i ^ 1) for i in range(shards)])
    across = lax.ppermute(projected, "shard", [(i, i ^ partner) for i in range(shards)])
    across_sibling = lax.ppermute(across, "shard", [(i, i ^ 1) for i in range(shards)])
    table = jnp.concatenate([projected, sibling, across, across_sibling], axis=0)

    def table_index(wanted):
        return ((wanted // item_dev) ^ my_code) * item_dev + wanted % item_dev

    summed = serve(
        server,
        server_rank,
        main_cap,
        table,
        table_index(received[:, :main_cap].reshape(-1)),
        server_rank < main_cap,
    )

    def spill(_):
        spill_rank = server_rank - main_cap
        wanted = received[:, main_cap:capacity].reshape(-1)
        return serve(
            server, spill_rank, spill_cap, table, table_index(wanted), spill_rank >= 0
        )

    def no_spill(_):
        return jnp.zeros_like(summed)

    summed = summed + lax.cond(region_crowded == 0, no_spill, spill, 0)
    aggregate = (summed / weight_sum).astype(jnp.bfloat16)
    activation = (
        jnp.dot(features, self_weight, preferred_element_type=jnp.float32)
        + jnp.dot(aggregate, nbr_weight, preferred_element_type=jnp.float32)
        + out_bias
    )
    activation = jnp.maximum(activation, 0.0)
    embedding = (
        activation * lax.rsqrt(jnp.mean(activation * activation, axis=-1, keepdims=True) + norm_eps)
    ).astype(jnp.bfloat16)

    items = jnp.arange(item_dev, dtype=jnp.int32)[None, :]
    query_pick = (query_ids[:, None] == items).astype(jnp.bfloat16)
    positive_pick = (positive_ids[:, None] == items).astype(jnp.bfloat16)
    query_emb = jnp.dot(query_pick, embedding, preferred_element_type=jnp.float32)
    positive_emb = jnp.dot(positive_pick, embedding, preferred_element_type=jnp.float32)
    positive_score = score_scale / hidden * jnp.sum(query_emb * positive_emb, axis=-1)
    neg_lists = neg_blocks[0]
    regions = lax.axis_size("region")
    here = lax.axis_index("region")
    arrived = [embedding] + [
        lax.ppermute(embedding, "region", [(r, (r + k) % regions) for r in range(regions)])
        for k in range(1, regions)
    ]
    scores = (
        score_scale
        / hidden
        * jnp.dot(
            query_emb.astype(jnp.bfloat16),
            jnp.concatenate(arrived, axis=0).T,
            preferred_element_type=jnp.float32,
        )
    )
    hinge_all = jnp.maximum(scores - positive_score[:, None] + margin_value, 0.0)
    block_mean = jnp.mean(hinge_all.reshape(query_emb.shape[0], -1, block_rows), axis=-1)
    per_region = block_mean.shape[1] // regions
    slot = ((here - neg_lists // per_region) % regions) * per_region + neg_lists % per_region
    pool_ids = jnp.arange(block_mean.shape[1], dtype=jnp.int32)
    picked = jnp.where(slot[None, :, None] == pool_ids[None, None, :], block_mean[:, None, :], 0.0)
    hinge_terms = jnp.sum(picked, axis=-1)
    return (embedding, hinge_terms)


def solution(mesh):
    in_specs = (
        P(("region", "shard"), None),
        P(),
        P(),
        P(),
        P(),
        P(),
        P(("region", "shard"), None),
        P(("region", "shard"), None),
        P(("region", "shard")),
        P(("region", "shard")),
        P(("region", "shard")),
        P(("region", "shard"), None),
    )
    out_specs = (P(("region", "shard"), None), P(("region", "shard"), None))
    return jax.shard_map(body, mesh=mesh, in_specs=in_specs, out_specs=out_specs, check_vma=False)
```

```python
import jax
import jax.numpy as jnp
from jax import lax
from jax.sharding import PartitionSpec as P

score_scale = 32.0
margin_value = 1.0
norm_eps = 1e-06


def exclusive_counts(onehot, chunk):
    n, m = onehot.shape
    blocks = n // chunk
    oh = onehot.reshape(blocks, chunk, m)
    ii = lax.broadcasted_iota(jnp.int32, (chunk, chunk), 0)
    jj = lax.broadcasted_iota(jnp.int32, (chunk, chunk), 1)
    tri = (jj < ii).astype(jnp.bfloat16)
    within = jnp.einsum("ij,bjo->bio", tri, oh, preferred_element_type=jnp.float32)
    totals = jnp.sum(oh.astype(jnp.float32), axis=1)
    bi = lax.broadcasted_iota(jnp.int32, (blocks, blocks), 0)
    bj = lax.broadcasted_iota(jnp.int32, (blocks, blocks), 1)
    btri = (bj < bi).astype(jnp.float32)
    offsets = jnp.dot(btri, totals, precision=lax.Precision.HIGHEST)
    return (within + offsets[:, None, :]).reshape(n, m)


def body(
    features,
    proj_weight,
    proj_bias,
    self_weight,
    nbr_weight,
    out_bias,
    nbr_ids,
    nbr_counts,
    live_slots,
    query_ids,
    positive_ids,
    neg_blocks,
):
    item_dev = features.shape[0]
    hidden = proj_weight.shape[1]
    fanout = nbr_ids.shape[1]
    block_rows = item_dev // live_slots.shape[0]
    shards = lax.axis_size("shard")
    slots = item_dev * fanout
    capacity = max(2, 2 * slots // shards)

    projected = jnp.maximum(
        jnp.dot(features, proj_weight, preferred_element_type=jnp.float32) + proj_bias, 0.0
    ).astype(jnp.bfloat16)

    live_item = jnp.repeat(live_slots, block_rows, total_repeat_length=item_dev)
    slot_weight = jnp.where(
        jnp.arange(fanout, dtype=jnp.int32)[None, :] < live_item[:, None], nbr_counts, 0
    )
    weight_sum = jnp.sum(slot_weight.astype(jnp.float32), axis=1, keepdims=True)

    flat_ids = nbr_ids.reshape(-1)
    owners = flat_ids // item_dev
    local_row = flat_ids % item_dev

    def make_requests(server, value, rank, cap):
        server_hot = server[:, None] == jnp.arange(shards, dtype=jnp.int32)[None, :]
        rank_hot = rank[:, None] == jnp.arange(cap, dtype=jnp.int32)[None, :]
        lo = jnp.where(rank_hot, (value % item_dev)[:, None].astype(jnp.float32), 0.0)
        hi = jnp.where(rank_hot, (value // item_dev)[:, None].astype(jnp.float32), 0.0)
        both = jnp.dot(
            server_hot.astype(jnp.bfloat16).T,
            jnp.concatenate([lo, hi], axis=1).astype(jnp.bfloat16),
            preferred_element_type=jnp.float32,
        ).astype(jnp.int32)
        return both[:, cap:] * item_dev + both[:, :cap]

    def serve(server, rank, cap, table, index, valid):
        pick = (index[:, None] == jnp.arange(table.shape[0], dtype=jnp.int32)[None, :]).astype(
            jnp.bfloat16
        )
        outgoing = jnp.dot(pick, table, preferred_element_type=jnp.float32).astype(jnp.bfloat16)
        outgoing = outgoing.reshape(shards, cap, hidden)
        incoming = lax.all_to_all(outgoing, "shard", split_axis=0, concat_axis=0, tiled=True)
        column = (server * cap + rank).reshape(item_dev, fanout)
        weight = jnp.where(valid.reshape(item_dev, fanout), slot_weight, 0)
        spread = jnp.where(
            column[:, :, None] == jnp.arange(shards * cap, dtype=jnp.int32)[None, None, :],
            weight[:, :, None].astype(jnp.float32),
            0.0,
        )
        mix = jnp.sum(spread, axis=1).astype(jnp.bfloat16)
        return jnp.dot(
            mix, incoming.reshape(shards * cap, hidden), preferred_element_type=jnp.float32
        )

    def rank_within(group, groups):
        hot = group[:, None] == jnp.arange(groups, dtype=jnp.int32)[None, :]
        counts = exclusive_counts(hot.astype(jnp.bfloat16), 128)
        rank = jnp.sum(jnp.where(hot, counts, 0.0), axis=1).astype(jnp.int32)
        totals = jnp.sum(hot.astype(jnp.float32), axis=0)
        return rank, totals

    partner = shards // 4
    members = 4
    groups = shards // members
    main_cap = capacity * 5 // 8
    spill_cap = capacity - main_cap
    low = owners % 2
    high = (owners // partner) % 2
    group = (owners // (2 * partner)) * (partner // 2) + (owners % partner) // 2
    group_rank, group_totals = rank_within(group, groups)
    crowded = (jnp.max(group_totals) > members * main_cap).astype(jnp.int32)
    turn = group_rank % members
    group_base = (owners // (2 * partner)) * (2 * partner) + (owners % partner) // 2 * 2
    server = group_base + (turn // 2) * partner + turn % 2
    server_rank = group_rank // members
    value = (high * 2 + low) * item_dev + local_row
    requests = make_requests(server, value, server_rank, capacity)
    flagged = jnp.concatenate([requests, jnp.broadcast_to(crowded, (shards, 1))], axis=1)
    received = lax.all_to_all(flagged, "shard", split_axis=0, concat_axis=0, tiled=True)
    region_crowded = jnp.max(received[:, capacity])
    me = lax.axis_index("shard")
    my_code = ((me // partner) % 2) * 2 + me % 2
    sibling = lax.ppermute(projected, "shard", [(i, i ^ 1) for i in range(shards)])
    across = lax.ppermute(projected, "shard", [(i, i ^ partner) for i in range(shards)])
    across_sibling = lax.ppermute(across, "shard", [(i, i ^ 1) for i in range(shards)])
    table = jnp.concatenate([projected, sibling, across, across_sibling], axis=0)

    def table_index(wanted):
        return ((wanted // item_dev) ^ my_code) * item_dev + wanted % item_dev

    summed = serve(
        server,
        server_rank,
        main_cap,
        table,
        table_index(received[:, :main_cap].reshape(-1)),
        server_rank < main_cap,
    )

    def spill(_):
        spill_rank = server_rank - main_cap
        wanted = received[:, main_cap:capacity].reshape(-1)
        return serve(
            server, spill_rank, spill_cap, table, table_index(wanted), spill_rank >= 0
        )

    def no_spill(_):
        return jnp.zeros_like(summed)

    summed = summed + lax.cond(region_crowded == 0, no_spill, spill, 0)
    aggregate = (summed / weight_sum).astype(jnp.bfloat16)
    activation = (
        jnp.dot(features, self_weight, preferred_element_type=jnp.float32)
        + jnp.dot(aggregate, nbr_weight, preferred_element_type=jnp.float32)
        + out_bias
    )
    activation = jnp.maximum(activation, 0.0)
    embedding = (
        activation * lax.rsqrt(jnp.mean(activation * activation, axis=-1, keepdims=True) + norm_eps)
    ).astype(jnp.bfloat16)

    items = jnp.arange(item_dev, dtype=jnp.int32)[None, :]
    query_pick = (query_ids[:, None] == items).astype(jnp.bfloat16)
    positive_pick = (positive_ids[:, None] == items).astype(jnp.bfloat16)
    query_emb = jnp.dot(query_pick, embedding, preferred_element_type=jnp.float32)
    positive_emb = jnp.dot(positive_pick, embedding, preferred_element_type=jnp.float32)
    positive_score = score_scale / hidden * jnp.sum(query_emb * positive_emb, axis=-1)
    neg_lists = neg_blocks[0]
    regions = lax.axis_size("region")
    here = lax.axis_index("region")
    def shift(x, k):
        return lax.ppermute(x, "region", [(r, (r + k) % regions) for r in range(regions)])

    split = item_dev // 2
    from_left = shift(embedding, 1)
    from_right = shift(jnp.concatenate([embedding, embedding[split:]], axis=0), -1)
    relayed = shift(from_right[item_dev:], -1)
    direct = shift(embedding[:split], 2)
    arrived = [
        embedding,
        from_left,
        jnp.concatenate([direct, relayed], axis=0),
        from_right[:item_dev],
    ]
    scores = (
        score_scale
        / hidden
        * jnp.dot(
            query_emb.astype(jnp.bfloat16),
            jnp.concatenate(arrived, axis=0).T,
            preferred_element_type=jnp.float32,
        )
    )
    hinge_all = jnp.maximum(scores - positive_score[:, None] + margin_value, 0.0)
    block_mean = jnp.mean(hinge_all.reshape(query_emb.shape[0], -1, block_rows), axis=-1)
    per_region = block_mean.shape[1] // regions
    slot = ((here - neg_lists // per_region) % regions) * per_region + neg_lists % per_region
    pool_ids = jnp.arange(block_mean.shape[1], dtype=jnp.int32)
    picked = jnp.where(slot[None, :, None] == pool_ids[None, None, :], block_mean[:, None, :], 0.0)
    hinge_terms = jnp.sum(picked, axis=-1)
    return (embedding, hinge_terms)


def solution(mesh):
    in_specs = (
        P(("region", "shard"), None),
        P(),
        P(),
        P(),
        P(),
        P(),
        P(("region", "shard"), None),
        P(("region", "shard"), None),
        P(("region", "shard")),
        P(("region", "shard")),
        P(("region", "shard")),
        P(("region", "shard"), None),
    )
    out_specs = (P(("region", "shard"), None), P(("region", "shard"), None))
    return jax.shard_map(body, mesh=mesh, in_specs=in_specs, out_specs=out_specs, check_vma=False)
```
